32 devices in a mesh: groups: 2 (over x), tensor: 16 (over z, y, core).
Axes of the slice: x: 2, y: 2, z: 4, core: 2. Of those that a mesh axis runs over, the one named last changes fastest.
Arguments:
- tokens: bfloat16 [1024, 8192], P('groups', 'tensor'), parts along dimension 0, may hold values from -6 to 6
- norm_gain: float32 [8192], P('tensor'), may hold values from 0.1 to 1.9
- w_in: bfloat16 [8192, 3, 8192], P(None, None, 'tensor'), may hold values from -0.0625 to 0.0625
- w_short: float32 [3, 3, 8192], P(None, None, 'tensor'), may hold values from -3 to 3
- filters: bfloat16 [512, 128], P('tensor'), may hold values from -0.5 to 0.5
- skip: float32 [8192], P('tensor'), may hold values from -4 to 4
- w_out: bfloat16 [8192, 8192], P('tensor'), may hold values from -0.0625 to 0.0625
Outputs:
- mixed: bfloat16 [1024, 8192], P('groups', 'tensor'), parts along dimension 0
The draws below stay inside these ranges and needn't reach their ends.
There are 2 independent parts, one for each index of `groups`. The reference program is written for one: setup_inputs(seed, part) draws one part's arguments, and reference() takes and returns one part's arrays. A program takes and returns all parts, laid end to end along the dimension named above; an argument that names none is the same for every part. Nothing has to cross between parts.
All inputs are finite; a program needn't handle non-finite values.
Results may differ from the reference program's by a relative error of at most 0.0085.
Values may be sent and summed in bfloat16 or wider, within the bound.
A program may use at most 192 MiB of HBM per device.

```python
import jax
import jax.numpy as jnp
from jax import lax

D = 8192
TAPS = 128
GROUP = 16
SHORT = 3
TOKENS = 512
FILTERS = 512


def draw_tokens(key, part):
    column = jnp.arange(D, dtype=jnp.float32) / (D - 1)
    scale = 0.5 * jnp.exp(jnp.log(3.0) * column)
    base = jax.random.truncated_normal(key, -4.0, 4.0, (TOKENS, D), jnp.float32)
    return (base * scale[None, :]).astype(jnp.bfloat16)


def shard_levels(rng, dims, shards, least, largest):
    level, own = 1.0, jax.random.fold_in(rng, 6)
    for position, parts in shards:
        steps = jnp.exp(jax.random.uniform(jax.random.fold_in(own, position), (parts,), jnp.float32, least / len(shards), largest / len(shards)))
        level = level * jnp.repeat(steps, dims[position] // parts).reshape([-1 if axis == position else 1 for axis in range(len(dims))])
    return level


def normal_values(key, shape, width, reach, split=(), kind=jnp.bfloat16):
    values = width * jax.random.normal(key, shape, jnp.float32)
    if split:
        values = values * shard_levels(key, shape, split, -0.22, 0.18)
    return jnp.clip(values, -reach, reach).astype(kind)


def setup_inputs(seed: int = 0, part: int = 0) -> dict:
    splits = jax.random.split(jax.random.key(seed), 8)
    part_keys = jax.random.split(jax.random.fold_in(splits[7], part), 8)
    return {
        "tokens": draw_tokens(jax.random.fold_in(jax.random.fold_in(splits[7], part), 71), part),
        "norm_gain": jnp.clip(1.0 + 0.18 * jax.random.normal(splits[1], (D,), jnp.float32), 0.1, 1.9),
        "w_in": normal_values(splits[2], (D, 3, D), D ** -0.5, 0.0625, ((2, 16),)),
        "w_short": normal_values(splits[3], (SHORT, 3, D), 0.6, 3.0, ((2, 16),), jnp.float32),
        "filters": normal_values(splits[4], (FILTERS, TAPS), 0.09, 0.5, ((0, 16),)),
        "skip": normal_values(splits[5], (D,), 1.0, 4.0, ((0, 16),), jnp.float32),
        "w_out": normal_values(splits[6], (D, D), D ** -0.5, 0.0625, ((0, 16),)),
    }


def shifted(field, lag):
    pads = ((lag, 0),) + ((0, 0),) * (field.ndim - 1)
    return jnp.pad(field, pads)[:field.shape[0]]

def reference(tokens, norm_gain, w_in, w_short, filters, skip, w_out):
    wide = tokens.astype(jnp.float32)
    factor = lax.rsqrt(lax.optimization_barrier(jnp.mean(wide * wide, axis=1, keepdims=True)) + 1e-05)
    normed = (wide * factor * norm_gain[None, :]).astype(jnp.bfloat16)
    proj = jnp.dot(normed, w_in.reshape(D, 3 * D), preferred_element_type=jnp.float32)
    proj = proj.reshape(TOKENS, 3, D)
    short = w_short[0][None] * proj
    for lag in range(1, SHORT):
        short = short + w_short[lag][None] * shifted(proj, lag)
    gated = (short[:, 1] * short[:, 2]).astype(jnp.bfloat16)
    gated_wide = gated.astype(jnp.float32)
    taps_wide = jnp.repeat(filters.astype(jnp.float32), GROUP, axis=0)
    padded = jnp.pad(gated_wide, ((TAPS, 0), (0, 0)))

    def add_tap(step, total):
        step = step.astype(jnp.int32)
        window = lax.dynamic_slice_in_dim(padded, (TAPS - step).astype(jnp.int32), TOKENS, 0)
        column = lax.dynamic_index_in_dim(taps_wide, step, 1, keepdims=False)
        return total + column[None, :] * window
    conv = lax.fori_loop(0, TAPS, add_tap, jnp.zeros((TOKENS, D), jnp.float32))
    hidden = ((conv + skip[None, :] * gated_wide) * short[:, 0]).astype(jnp.bfloat16)
    result = wide + jnp.dot(hidden, w_out, preferred_element_type=jnp.float32)
    return result.astype(jnp.bfloat16)
```

```python
import jax
import jax.numpy as jnp
from jax import lax
from jax.sharding import PartitionSpec as P

D = 8192


def shifted(field, lag):
    pads = ((lag, 0),) + ((0, 0),) * (field.ndim - 1)
    return jnp.pad(field, pads)[: field.shape[0]]


def lag_block(filters, block):
    count, taps = filters.shape
    rows = 2 * block
    length = taps + rows
    line = jnp.concatenate([filters, jnp.zeros((count, rows), filters.dtype)], axis=1)
    tiled = jnp.tile(line, (1, rows))[:, : rows * (length - 1)]
    return tiled.reshape(count, rows, length - 1)[:, :, block:rows]


def on_device(tokens, norm_gain, w_in, w_short, filters, skip, w_out):
    wide = tokens.astype(jnp.float32)
    squares = lax.psum(jnp.sum(wide * wide, axis=1, keepdims=True), "tensor")
    factor = lax.rsqrt(squares / D + 1e-05)
    scaled = (wide * norm_gain[None, :]).astype(jnp.bfloat16)
    local = w_in.shape[2]
    rows = tokens.shape[0]
    x = lax.all_gather(scaled, "tensor", axis=1, tiled=True)
    short = []
    for b in range(3):
        proj = jnp.dot(x, w_in[:, b], preferred_element_type=jnp.float32) * factor
        out = w_short[0, b][None] * proj
        for lag in range(1, w_short.shape[0]):
            out = out + w_short[lag, b][None] * shifted(proj, lag)
        short.append(out)
    q, k, v = short
    gated = (k * v).astype(jnp.bfloat16)
    count, taps = filters.shape
    group = local // count
    blocks = rows // taps
    lagged = lag_block(filters, taps)
    cells = gated.T.reshape(count, group, blocks, taps)
    before = jnp.pad(cells, ((0, 0), (0, 0), (1, 0), (0, 0)))[:, :, :blocks]
    pair = jnp.concatenate([before, cells], axis=3).reshape(count, group * blocks, 2 * taps)
    conv = jnp.einsum("fms,fst->fmt", pair, lagged, preferred_element_type=jnp.float32)
    conv = conv.reshape(local, rows).T
    hidden = ((conv + skip[None, :] * gated.astype(jnp.float32)) * q).astype(jnp.bfloat16)
    part = jnp.dot(hidden, w_out, preferred_element_type=jnp.float32).astype(jnp.bfloat16)
    summed = lax.psum_scatter(part, "tensor", scatter_dimension=1, tiled=True)
    return (wide + summed.astype(jnp.float32)).astype(jnp.bfloat16)


def solution(mesh):
    return jax.shard_map(
        on_device,
        mesh=mesh,
        in_specs=(
            P("groups", "tensor"),
            P("tensor"),
            P(None, None, "tensor"),
            P(None, None, "tensor"),
            P("tensor", None),
            P("tensor"),
            P("tensor", None),
        ),
        out_specs=P("groups", "tensor"),
        check_vma=False,
    )
```
